32 devices in a mesh: wide: 8 (over z, x), narrow: 4 (over y, core).
Axes of the slice: x: 2, y: 2, z: 4, core: 2. Of those that a mesh axis runs over, the one named last changes fastest.
Arguments:
- tokens: bfloat16 [21504, 768], P(('wide', 'narrow')), may hold values from -6 to 6
- encoded: bfloat16 [48, 1536, 768], P(None, 'wide', 'narrow'), may hold values from -6 to 6
- lengths: int32 [48], P('wide'), may hold values from 4 to 448, as said below
- enc_frames: int32 [48], P('wide'), may hold values from 750 to 1500, as said below
- cotangent: bfloat16 [21504, 768], P(('wide', 'narrow')), may hold values from -6 to 6
- attn_gain: bfloat16 [768], replicated, may hold values from 0.099609375 to 1.8984375
- attn_shift: bfloat16 [768], replicated, may hold values from -2.5 to 2.5
- query_weight: bfloat16 [768, 768], P(None, 'narrow'), may hold values from -0.21875 to 0.21875
- query_bias: bfloat16 [768], P('narrow'), may hold values from -2.5 to 2.5
- key_weight: bfloat16 [768, 768], P(None, 'narrow'), may hold values from -0.21875 to 0.21875
- value_weight: bfloat16 [768, 768], P(None, 'narrow'), may hold values from -0.21875 to 0.21875
- value_bias: bfloat16 [768], P('narrow'), may hold values from -2.5 to 2.5
- output_weight: bfloat16 [768, 768], P('narrow'), may hold values from -1.75 to 1.75
- output_bias: bfloat16 [768], replicated, may hold values from -2.5 to 2.5
- cross_gain: bfloat16 [768], replicated, may hold values from 0.099609375 to 1.8984375
- cross_shift: bfloat16 [768], replicated, may hold values from -2.5 to 2.5
- lookup_weight: bfloat16 [768, 768], P(None, 'narrow'), may hold values from -0.21875 to 0.21875
- lookup_bias: bfloat16 [768], P('narrow'), may hold values from -2.5 to 2.5
- source_keys: bfloat16 [768, 768], P(None, 'narrow'), may hold values from -0.21875 to 0.21875
- source_values: bfloat16 [768, 768], P(None, 'narrow'), may hold values from -0.21875 to 0.21875
- source_bias: bfloat16 [768], P('narrow'), may hold values from -2.5 to 2.5
- merged_weight: bfloat16 [768, 768], P('narrow'), may hold values from -3.5 to 3.5
- merged_bias: bfloat16 [768], replicated, may hold values from -2.5 to 2.5
- dense_gain: bfloat16 [768], replicated, may hold values from 0.099609375 to 1.8984375
- dense_shift: bfloat16 [768], replicated, may hold values from -2.5 to 2.5
- expand_weight: bfloat16 [768, 3072], P(None, 'narrow'), may hold values from -0.21875 to 0.21875
- expand_bias: bfloat16 [3072], P('narrow'), may hold values from -2.5 to 2.5
- reduce_weight: bfloat16 [3072, 768], P('narrow'), may hold values from -0.109375 to 0.109375
- reduce_bias: bfloat16 [768], replicated, may hold values from -2.5 to 2.5
Outputs:
- result: bfloat16 [21504, 768], P(('wide', 'narrow'))
- tokens_grad: bfloat16 [21504, 768], P(('wide', 'narrow'))
- encoded_grad: bfloat16 [48, 1536, 768], P(None, 'wide', 'narrow')
- attn_gain_grad: float32 [768], replicated
- attn_shift_grad: float32 [768], replicated
- query_weight_grad: float32 [768, 768], P(None, 'narrow')
- query_bias_grad: float32 [768], P('narrow')
- key_weight_grad: float32 [768, 768], P(None, 'narrow')
- value_weight_grad: float32 [768, 768], P(None, 'narrow')
- value_bias_grad: float32 [768], P('narrow')
- output_weight_grad: float32 [768, 768], P('narrow')
- output_bias_grad: float32 [768], replicated
- cross_gain_grad: float32 [768], replicated
- cross_shift_grad: float32 [768], replicated
- lookup_weight_grad: float32 [768, 768], P(None, 'narrow')
- lookup_bias_grad: float32 [768], P('narrow')
- source_keys_grad: float32 [768, 768], P(None, 'narrow')
- source_values_grad: float32 [768, 768], P(None, 'narrow')
- source_bias_grad: float32 [768], P('narrow')
- merged_weight_grad: float32 [768, 768], P('narrow')
- merged_bias_grad: float32 [768], replicated
- dense_gain_grad: float32 [768], replicated
- dense_shift_grad: float32 [768], replicated
- expand_weight_grad: float32 [768, 3072], P(None, 'narrow')
- expand_bias_grad: float32 [3072], P('narrow')
- reduce_weight_grad: float32 [3072, 768], P('narrow')
- reduce_bias_grad: float32 [768], replicated
The draws below stay inside these ranges and needn't reach their ends.
Inputs may be any that keep to these rules, and one draw needn't show every extreme that they name: Items fall into three task groups: transcription items with lengths from 224, translation items from 112, and language-id items of at most 56 positions; item 0 has 448. `enc_frames`: item 0 has 1500 live frames.
All inputs are finite; a program needn't handle non-finite values.
Results may differ from the reference program's by a relative error of at most 0.02.
Values may be sent and summed in bfloat16 or wider, within the bound.
A program may use at most 384 MiB of HBM per device.

```python
import jax
import jax.numpy as jnp
from jax import lax

D = 768
HEADS = 12
HDIM = 64
FF = 3072
LEN = 448
ENCODED = 1500
FRAMES = 1536
ITEMS = 48
TOKENS = 21504


def draw_lengths(key, part):
    group_key, long_key, middle_key, short_key = jax.random.split(jax.random.fold_in(key, 11), 4)
    group = jax.random.randint(group_key, (ITEMS,), 0, 10)
    longer = jax.random.randint(long_key, (ITEMS,), LEN // 2, LEN + 1)
    middle = jax.random.randint(middle_key, (ITEMS,), LEN // 4, LEN + 1)
    shorter = jax.random.randint(short_key, (ITEMS,), 4, LEN // 8 + 1)
    drawn = jnp.where(group < 6, longer, jnp.where(group < 9, middle, shorter))
    return jnp.where(jnp.arange(ITEMS) == 0, LEN, drawn).astype(jnp.int32)


def draw_enc_frames(key, part):
    drawn = jax.random.randint(jax.random.fold_in(key, 23), (ITEMS,), ENCODED // 2, ENCODED + 1)
    return jnp.where(jnp.arange(ITEMS) == 0, ENCODED, drawn).astype(jnp.int32)


def block_scale(key, extent, cuts, low, top_value):
    def one(axis_at, blocks):
        draws = jax.random.uniform(jax.random.fold_in(jax.random.fold_in(key, 6), axis_at), (blocks,), jnp.float32, low / len(cuts), top_value / len(cuts))
        return jnp.repeat(jnp.exp(draws), extent[axis_at] // blocks).reshape((-1,) + (1,) * (len(extent) - axis_at - 1))

    factor_of = one(*cuts[0])
    for cut in cuts[1:]:
        factor_of = factor_of * one(*cut)
    return factor_of


def bell_draw(own_key, extent, scale, bound, shards=(), held_as=jnp.bfloat16):
    level = block_scale(own_key, extent, shards, -0.22, 0.18) if shards else 1.0
    entries = jax.random.normal(own_key, extent, jnp.float32) * scale * level
    return jnp.minimum(jnp.maximum(entries, -bound), bound).astype(held_as)


def setup_inputs(seed: int = 0) -> dict:
    splits = jax.random.split(jax.random.key(seed), 30)
    return {
        "tokens": bell_draw(splits[0], (TOKENS, D), 1.0, 6.0, ((0, 32),)),
        "encoded": bell_draw(splits[1], (ITEMS, FRAMES, D), 1.0, 6.0, ((1, 8), (2, 4))),
        "lengths": draw_lengths(jax.random.fold_in(splits[29], 71), 0),
        "enc_frames": draw_enc_frames(jax.random.fold_in(splits[29], 71), 0),
        "cotangent": bell_draw(splits[4], (TOKENS, D), 1.0, 6.0, ((0, 32),)),
        "attn_gain": jnp.clip(1.0 + 0.18 * jax.random.normal(splits[5], (D,), jnp.float32), 0.099609375, 1.8984375).astype(jnp.bfloat16),
        "attn_shift": bell_draw(splits[6], (D,), 0.5, 2.5),
        "query_weight": bell_draw(splits[7], (D, D), D ** -0.5, 0.21875, ((1, 4),)),
        "query_bias": bell_draw(splits[8], (D,), 0.5, 2.5, ((0, 4),)),
        "key_weight": bell_draw(splits[9], (D, D), D ** -0.5, 0.21875, ((1, 4),)),
        "value_weight": bell_draw(splits[10], (D, D), D ** -0.5, 0.21875, ((1, 4),)),
        "value_bias": bell_draw(splits[11], (D,), 0.5, 2.5, ((0, 4),)),
        "output_weight": bell_draw(splits[12], (D, D), (max(D // 64, 1)) ** -0.5, 1.75, ((0, 4),)),
        "output_bias": bell_draw(splits[13], (D,), 0.5, 2.5),
        "cross_gain": jnp.clip(1.0 + 0.18 * jax.random.normal(splits[14], (D,), jnp.float32), 0.099609375, 1.8984375).astype(jnp.bfloat16),
        "cross_shift": bell_draw(splits[15], (D,), 0.5, 2.5),
        "lookup_weight": bell_draw(splits[16], (D, D), D ** -0.5, 0.21875, ((1, 4),)),
        "lookup_bias": bell_draw(splits[17], (D,), 0.5, 2.5, ((0, 4),)),
        "source_keys": bell_draw(splits[18], (D, D), D ** -0.5, 0.21875, ((1, 4),)),
        "source_values": bell_draw(splits[19], (D, D), D ** -0.5, 0.21875, ((1, 4),)),
        "source_bias": bell_draw(splits[20], (D,), 0.5, 2.5, ((0, 4),)),
        "merged_weight": bell_draw(splits[21], (D, D), (max(D // 256, 1)) ** -0.5, 3.5, ((0, 4),)),
        "merged_bias": bell_draw(splits[22], (D,), 0.5, 2.5),
        "dense_gain": jnp.clip(1.0 + 0.18 * jax.random.normal(splits[23], (D,), jnp.float32), 0.099609375, 1.8984375).astype(jnp.bfloat16),
        "dense_shift": bell_draw(splits[24], (D,), 0.5, 2.5),
        "expand_weight": bell_draw(splits[25], (D, FF), D ** -0.5, 0.21875, ((1, 4),)),
        "expand_bias": bell_draw(splits[26], (FF,), 0.5, 2.5, ((0, 4),)),
        "reduce_weight": bell_draw(splits[27], (FF, D), FF ** -0.5, 0.109375, ((0, 4),)),
        "reduce_bias": bell_draw(splits[28], (D,), 0.5, 2.5),
    }


@jax.custom_vjp
def low(v):
    return lax.optimization_barrier(v.astype(jnp.bfloat16)).astype(jnp.float32)

@jax.custom_vjp
def low_back(v):
    return v

def low_keep(v):
    return (low(v), None)

def low_pass(kept, grad):
    return (grad,)

def back_keep(v):
    return (v, None)

def back_low(kept, grad):
    return (low(grad),)
low.defvjp(low_keep, low_pass)
low_back.defvjp(back_keep, back_low)

def matmul(left, right):
    return jnp.matmul(left, right, precision=lax.Precision.HIGHEST)

def layer_norm(values, gain, shift):
    center = values - lax.optimization_barrier(jnp.mean(values, axis=-1, keepdims=True))
    spread = lax.optimization_barrier(jnp.mean(center * center, axis=-1, keepdims=True))
    return center * lax.rsqrt(spread + 1e-05) * gain + shift

def rounded(values):
    return low_back(low(values))

def attend(query, keys, values, allowed):
    batch, rows, width = query.shape
    frames = keys.shape[1]
    query_heads = query.reshape(batch, rows, HEADS, HDIM)
    key_heads = keys.reshape(batch, frames, HEADS, HDIM)
    value_heads = values.reshape(batch, frames, HEADS, HDIM)
    raw = jnp.einsum('blhe,bshe->bhls', query_heads, key_heads, precision=lax.Precision.HIGHEST)
    scores = jnp.where(allowed, low_back(raw * HDIM ** (-0.5)), -1e+30)
    largest = lax.optimization_barrier(jnp.max(scores, axis=-1, keepdims=True))
    expos = jnp.exp(scores - largest)
    probs = low(expos / lax.optimization_barrier(jnp.sum(expos, axis=-1, keepdims=True)))
    mixed = jnp.einsum('bhls,bshe->blhe', probs, value_heads, precision=lax.Precision.HIGHEST)
    return mixed.reshape(batch, rows, width)

def block(params, rows, source, lens, frames):
    attn_gain, attn_shift, query_weight, query_bias, key_weight, value_weight, value_bias, output_weight, output_bias, cross_gain, cross_shift, lookup_weight, lookup_bias, source_keys, source_values, source_bias, merged_weight, merged_bias, dense_gain, dense_shift, expand_weight, expand_bias, reduce_weight, reduce_bias = params
    places = jnp.arange(LEN)
    causal = (places[None, :] <= places[:, None])[None, None] & (places[None, None, None, :] < lens[:, None, None, None])
    heard = jnp.arange(FRAMES)[None, None, None, :] < frames[:, None, None, None]
    first = low(layer_norm(rows, attn_gain, attn_shift))
    query = rounded(matmul(first, query_weight) + query_bias)
    keys = rounded(matmul(first, key_weight))
    values = rounded(matmul(first, value_weight) + value_bias)
    attended = rounded(attend(query, keys, values, causal))
    after_self = rows + low_back(matmul(attended, output_weight)) + output_bias
    second = low(layer_norm(after_self, cross_gain, cross_shift))
    lookup = rounded(matmul(second, lookup_weight) + lookup_bias)
    heard_keys = rounded(matmul(source, source_keys))
    heard_values = rounded(matmul(source, source_values) + source_bias)
    recalled = rounded(attend(lookup, heard_keys, heard_values, heard))
    after_cross = after_self + low_back(matmul(recalled, merged_weight)) + merged_bias
    third = low(layer_norm(after_cross, dense_gain, dense_shift))
    widened = low_back(matmul(third, expand_weight) + expand_bias)
    activated = low(jax.nn.gelu(widened, approximate=False))
    return after_cross + low_back(matmul(activated, reduce_weight)) + reduce_bias

def reference(tokens, encoded, lengths, enc_frames, cotangent, attn_gain, attn_shift, query_weight, query_bias, key_weight, value_weight, value_bias, output_weight, output_bias, cross_gain, cross_shift, lookup_weight, lookup_bias, source_keys, source_values, source_bias, merged_weight, merged_bias, dense_gain, dense_shift, expand_weight, expand_bias, reduce_weight, reduce_bias):
    raw_params = (attn_gain, attn_shift, query_weight, query_bias, key_weight, value_weight, value_bias, output_weight, output_bias, cross_gain, cross_shift, lookup_weight, lookup_bias, source_keys, source_values, source_bias, merged_weight, merged_bias, dense_gain, dense_shift, expand_weight, expand_bias, reduce_weight, reduce_bias)
    params = tuple((member.astype(jnp.float32) for member in raw_params))
    groups = ITEMS // 4
    hidden = tokens.astype(jnp.float32).reshape(groups, 4, LEN, D)
    memory = encoded.astype(jnp.float32).reshape(groups, 4, FRAMES, D)
    lens = lengths.reshape(groups, 4)
    frames = enc_frames.reshape(groups, 4)
    upstream_rows = cotangent.astype(jnp.float32).reshape(groups, 4, LEN, D)

    def group_step(totals, inputs):
        rows, source, lens_group, frames_group, upstream = inputs

        def forward(weights, rows_in, source_in):
            return block(weights, rows_in, source_in, lens_group, frames_group)
        output, pull = jax.vjp(forward, params, rows, source)
        weight_grads, row_grads, source_grads = pull(upstream)
        totals = jax.tree.map(jnp.add, totals, weight_grads)
        return (totals, (output, row_grads, source_grads))
    start = jax.tree.map(jnp.zeros_like, params)
    totals, (outputs, row_grads, source_grads) = lax.scan(group_step, start, (hidden, memory, lens, frames, upstream_rows))
    result = outputs.reshape(TOKENS, D).astype(jnp.bfloat16)
    tokens_grad = row_grads.reshape(TOKENS, D).astype(jnp.bfloat16)
    encoded_grad = source_grads.reshape(ITEMS, FRAMES, D).astype(jnp.bfloat16)
    return (result, tokens_grad, encoded_grad, totals[0], totals[1], totals[2], totals[3], totals[4], totals[5], totals[6], totals[7], totals[8], totals[9], totals[10], totals[11], totals[12], totals[13], totals[14], totals[15], totals[16], totals[17], totals[18], totals[19], totals[20], totals[21], totals[22], totals[23])
```

```python
import functools
import math

import jax
import jax.numpy as jnp
from jax import lax
from jax.experimental import pallas as pl
from jax.experimental.pallas import tpu as pltpu
from jax.sharding import PartitionSpec as P

HDIM=64
NEG=-1e30
SCALE=HDIM**-0.5
LOG2E=math.log2(math.e)
C=SCALE*LOG2E
NT=(((1,),(1,)),((),()))
TN=(((0,),(0,)),((),()))
NN=(((1,),(0,)),((),()))
def _dot(a,b,dims): return lax.dot_general(a,b,dims,preferred_element_type=jnp.float32)

def _masked(s, causal, off, live, base):
    col=lax.broadcasted_iota(jnp.int32,s.shape,1)
    ok=col<live
    if causal:
        row=lax.broadcasted_iota(jnp.int32,s.shape,0)+off
        ok=ok&(col<=row)
    return jnp.where(ok,s,NEG)

def fwd_kernel(off_ref, live_ref, q_ref, kv_ref, o_ref, l_ref, *, causal):
    j=pl.program_id(1)
    off=off_ref[j]; live=live_ref[j]
    bq=q_ref.shape[0]; S=kv_ref.shape[0]
    low=lax.broadcasted_iota(jnp.int32,(bq,128),1)<HDIM
    lowv=lax.broadcasted_iota(jnp.int32,(S,128),1)<HDIM
    one=jnp.ones((S,128),jnp.bfloat16)
    zq=jnp.zeros((bq,128),jnp.bfloat16)
    for g in range(q_ref.shape[1]//128):
        lanes=slice(128*g,128*g+128)
        q=q_ref[:,lanes]
        k=kv_ref[:,256*g:256*g+128]; v=kv_ref[:,256*g+128:256*g+256]
        accs=[];tops=[]
        for h in (0,1):
            mine=low if h==0 else ~low
            minev=lowv if h==0 else ~lowv
            s=_masked(_dot(jnp.where(mine,q,zq),k,NT),causal,off,live,0)
            top=jnp.max(s,axis=1,keepdims=True)
            p=jnp.exp2((s-top)*C).astype(jnp.bfloat16)
            accs.append(_dot(p,jnp.where(minev,v,one),NN))
            tops.append(top)
        total=pltpu.roll(jnp.where(low,accs[1],accs[0]),HDIM,1)
        o_ref[:,lanes]=(jnp.where(low,accs[0],accs[1])/total).astype(o_ref.dtype)
        l_ref[:,lanes]=jnp.where(low,tops[0],tops[1])*C+jnp.log2(total)

def attn_fwd(q, kv, off, live, *, causal, bq, nq, q0, item_of, S, hb=1, vmem=56<<20):
    heads2=q.shape[1]//128//hb
    rows=bq*nq
    return pl.pallas_call(
        functools.partial(fwd_kernel,causal=causal),
        out_shape=(jax.ShapeDtypeStruct((rows,q.shape[1]),jnp.bfloat16),jax.ShapeDtypeStruct((rows,q.shape[1]),jnp.float32)),
        grid_spec=pltpu.PrefetchScalarGridSpec(num_scalar_prefetch=2,grid=(heads2,nq),
            in_specs=[pl.BlockSpec((bq,128*hb),lambda h,j,*_:(q0+j,h)),
                      pl.BlockSpec((S,256*hb),lambda h,j,*_:(item_of(j),h))],
            out_specs=(pl.BlockSpec((bq,128*hb),lambda h,j,*_:(j,h)),pl.BlockSpec((bq,128*hb),lambda h,j,*_:(j,h)))),
        compiler_params=pltpu.CompilerParams(dimension_semantics=("arbitrary","arbitrary"),vmem_limit_bytes=vmem),
        cost_estimate=pl.CostEstimate(flops=hb*heads2*nq*8*bq*S*128,transcendentals=hb*heads2*nq*2*bq*S,bytes_accessed=rows*768*8+S*1536*2),
    )(off,live,q,kv)

def bwd_kernel(off_ref, live_ref, q_ref, kv_ref, do_ref, o_ref, l_ref, dq_ref, dkv_ref, acc_ref, *, causal, first, last, nq):
    j=pl.program_id(1)
    off=off_ref[j]; live=live_ref[j]
    bq=q_ref.shape[0]; S=kv_ref.shape[0]
    low=lax.broadcasted_iota(jnp.int32,(bq,128),1)<HDIM
    lowv=lax.broadcasted_iota(jnp.int32,(S,128),1)<HDIM
    zq=jnp.zeros((bq,128),jnp.bfloat16); zv=jnp.zeros((S,128),jnp.bfloat16)
    is_first=functools.reduce(jnp.logical_or,[j==f for f in first])
    is_last=functools.reduce(jnp.logical_or,[j==f for f in last])
    for g in range(q_ref.shape[1]//128):
        lanes=slice(128*g,128*g+128)
        lk=slice(256*g,256*g+128); lv=slice(256*g+128,256*g+256)
        q=q_ref[:,lanes]; do=do_ref[:,lanes]
        k=kv_ref[:,lk]; v=kv_ref[:,lv]
        prod=do.astype(jnp.float32)*o_ref[:,lanes].astype(jnp.float32)
        stat=l_ref[:,lanes]
        dq=None;dk=None;dv=None
        for h in (0,1):
            mine=low if h==0 else ~low
            minev=lowv if h==0 else ~lowv
            qh=jnp.where(mine,q,zq); doh=jnp.where(mine,do,zq)
            kh=jnp.where(minev,k,zv)
            s=_masked(_dot(qh,k,NT),causal,off,live,0)
            p=jnp.exp2(s*C-stat[:,h*HDIM:h*HDIM+1])
            dp=_dot(doh,v,NT)
            D=jnp.sum(jnp.where(mine,prod,0.0),axis=1,keepdims=True)
            ds=(p*(dp-D)).astype(jnp.bfloat16)
            pb=p.astype(jnp.bfloat16)
            a=_dot(ds,kh,NN); b=_dot(ds,qh,TN); c=_dot(pb,doh,TN)
            dq=a if dq is None else dq+a
            dk=b if dk is None else dk+b
            dv=c if dv is None else dv+c
        dq_ref[:,lanes]=(dq*SCALE).astype(dq_ref.dtype)
        dk=dk*SCALE
        if len(first)==nq:
            dkv_ref[:,lk]=dk.astype(dkv_ref.dtype); dkv_ref[:,lv]=dv.astype(dkv_ref.dtype)
        else:
            @pl.when(is_first)
            def _():
                acc_ref[:,lk]=dk; acc_ref[:,lv]=dv
            @pl.when(jnp.logical_not(is_first))
            def _():
                acc_ref[:,lk]+=dk; acc_ref[:,lv]+=dv
    if len(first)!=nq:
        @pl.when(is_last)
        def _():
            dkv_ref[...]=acc_ref[...].astype(dkv_ref.dtype)

def attn_bwd(q, kv, do, o, stat, off, live, *, causal, bq, nq, q0, do0, s0, item_of, items, first, last, S, hb=1, vmem=60<<20):
    heads2=q.shape[1]//128//hb
    rows=bq*nq
    return pl.pallas_call(
        functools.partial(bwd_kernel,causal=causal,first=first,last=last,nq=nq),
        out_shape=(jax.ShapeDtypeStruct((rows,q.shape[1]),jnp.bfloat16),jax.ShapeDtypeStruct((items*S,2*q.shape[1]),jnp.bfloat16)),
        grid_spec=pltpu.PrefetchScalarGridSpec(num_scalar_prefetch=2,grid=(heads2,nq),
            in_specs=[pl.BlockSpec((bq,128*hb),lambda h,j,*_:(q0+j,h)),
                      pl.BlockSpec((S,256*hb),lambda h,j,*_:(item_of(j),h)),
                      pl.BlockSpec((bq,128*hb),lambda h,j,*_:(do0+j,h)),
                      pl.BlockSpec((bq,128*hb),lambda h,j,*_:(do0+j,h)),
                      pl.BlockSpec((bq,128*hb),lambda h,j,*_:(s0+j,h))],
            out_specs=(pl.BlockSpec((bq,128*hb),lambda h,j,*_:(j,h)),pl.BlockSpec((S,256*hb),lambda h,j,*_:(item_of(j),h))),
            scratch_shapes=[pltpu.VMEM((S if len(first)!=nq else 8,256*hb),jnp.float32)]),
        compiler_params=pltpu.CompilerParams(dimension_semantics=("arbitrary","arbitrary"),vmem_limit_bytes=vmem),
        cost_estimate=pl.CostEstimate(flops=hb*heads2*nq*20*bq*S*128,transcendentals=hb*heads2*nq*2*bq*S,bytes_accessed=rows*768*12+S*1536*4),
    )(off,live,q,kv,do,o,stat)


LEN = 448
HALF = LEN // 2
BF = jnp.bfloat16
F32 = jnp.float32


def mm(a, b, dims):
    return lax.dot_general(a, b, dims, preferred_element_type=F32)


def norm_parts(values):
    center = values - jnp.mean(values, axis=-1, keepdims=True)
    scaled = lax.rsqrt(jnp.mean(center * center, axis=-1, keepdims=True) + 1e-05)
    return center * scaled, scaled


def norm_apply(normal, gain, shift):
    return (normal * gain.astype(F32) + shift.astype(F32)).astype(BF)


def norm_backward(grad, normal, scaled, gain):
    weighted = grad * gain.astype(F32)
    centered = weighted - jnp.mean(weighted, axis=-1, keepdims=True)
    return scaled * (centered - normal * jnp.mean(weighted * normal, axis=-1, keepdims=True))


def interleave(first, second):
    pairs = first.shape[0] // 128
    tail = first.shape[1:]
    return jnp.stack(
        [first.reshape((pairs, 128) + tail), second.reshape((pairs, 128) + tail)], axis=1
    ).reshape((2 * first.shape[0],) + tail)


def separate(both):
    tail = both.shape[1:]
    split = both.reshape((both.shape[0] // 256, 2, 128) + tail)
    flat = (both.shape[0] // 2,) + tail
    return split[:, 0].reshape(flat), split[:, 1].reshape(flat)


def make_body(wide, narrow):
    beside = [(i, i ^ 1) for i in range(narrow)]
    across = [(i, i ^ 2) for i in range(narrow)]

    def on_device(
        tokens,
        encoded,
        lengths,
        enc_frames,
        cotangent,
        attn_gain,
        attn_shift,
        query_weight,
        query_bias,
        key_weight,
        value_weight,
        value_bias,
        output_weight,
        output_bias,
        cross_gain,
        cross_shift,
        lookup_weight,
        lookup_bias,
        source_keys,
        source_values,
        source_bias,
        merged_weight,
        merged_bias,
        dense_gain,
        dense_shift,
        expand_weight,
        expand_bias,
        reduce_weight,
        reduce_bias,
    ):
        rows, width = tokens.shape
        part = width // narrow
        own_frames = encoded.shape[1]
        frames = own_frames * wide
        n = lax.axis_index("narrow")
        odd = lax.rem(n, 2)
        chip = lax.div(n, 2)
        is_odd = odd == 1

        def swap(values):
            return lax.ppermute(values, "narrow", beside)

        def gather(values):
            return lax.all_gather(values, "narrow", axis=0, tiled=True)

        def arrange(values):
            return jnp.where(is_odd, jnp.concatenate([values[HALF:], values[:HALF]]), values)

        def restore(values):
            return jnp.where(is_odd, jnp.concatenate([values[LEN:], values[:LEN]]), values)

        def stacked_gather(parts):
            count = len(parts)
            got = lax.all_gather(jnp.stack(parts), "narrow", axis=0, tiled=False)
            return [got[:, i].reshape(width, width) for i in range(count)]

        query_t, key_t, value_t = stacked_gather([query_weight.T, key_weight.T, value_weight.T])
        output_w, lookup_t, keys_t, values_t, merged_w = stacked_gather(
            [output_weight, lookup_weight.T, source_keys.T, source_values.T, merged_weight]
        )
        expand_t = gather(expand_weight.T)
        reduce_w = gather(reduce_weight)
        biases = lax.all_gather(
            jnp.stack([query_bias, value_bias, lookup_bias, source_bias]), "narrow", axis=1, tiled=True
        ).astype(F32)
        query_b, value_b, lookup_b, source_b = biases[0], biases[1], biases[2], biases[3]
        expand_b = gather(expand_bias).astype(F32)

        mine_in = []
        grouped = encoded.reshape(wide, 2, 3, own_frames, part)
        kept = lax.dynamic_index_in_dim(grouped, chip, 1, keepdims=False)
        sent = lax.dynamic_index_in_dim(grouped, 1 - chip, 1, keepdims=False)
        halfway = own_frames // 2

        def pack(values):
            return jnp.concatenate([values[..., :halfway, :], values[..., halfway:, :]], -1)

        def unpack(values):
            return jnp.concatenate([values[..., :part], values[..., part:]], -2)

        def spread(values):
            return lax.all_to_all(values, "wide", split_axis=0, concat_axis=0, tiled=True)

        def arrive(c):
            got = unpack(lax.ppermute(pack(sent[:, c]), "narrow", across))
            both = jnp.concatenate([kept[:, c], got], -1)
            return spread(both).reshape(frames, 2 * part)

        shared_own = arrive(1)
        first_own = arrive(0)
        last_own = arrive(2)
        shared = jnp.concatenate([shared_own, swap(shared_own)], -1)
        full = jnp.concatenate(
            [
                jnp.where(is_odd, last_own, first_own),
                swap(jnp.where(is_odd, first_own, last_own)),
            ],
            -1,
        )
        order = [n, n ^ 2, n ^ 1, n ^ 3]
        source_t = interleave(keys_t, values_t)
        columns = source_t.reshape(2 * width, narrow, part)
        source_w = jnp.concatenate(
            [lax.dynamic_index_in_dim(columns, o, 1, keepdims=False) for o in order], -1
        )
        source_bb = interleave(jnp.zeros_like(source_b), source_b)

        item_full = 3 * chip + 2 * odd
        item_half = 3 * chip + 1
        len_full, len_half = lengths[item_full], lengths[item_half]
        live_full, live_half = enc_frames[item_full], enc_frames[item_half]
        zero = jnp.int32(0)

        rows_in = arrange(tokens)
        half_own = rows_in[LEN:]
        half_got = swap(half_own)
        extended = jnp.concatenate(
            [
                rows_in[:LEN],
                jnp.where(is_odd, half_got, half_own),
                jnp.where(is_odd, half_own, half_got),
            ]
        ).astype(F32)
        normal_ext, unused = norm_parts(extended)
        first_ext = norm_apply(normal_ext, attn_gain, attn_shift)
        rows_in = rows_in.astype(F32)
        normal_self, scaled_self = norm_parts(rows_in)
        first = norm_apply(normal_self, attn_gain, attn_shift)
        pair_t = interleave(key_t, value_t)
        pair_b = interleave(jnp.zeros_like(value_b), value_b)
        query = (mm(first, query_t, NT) + query_b).astype(BF)
        pair = (mm(first_ext, pair_t, NT) + pair_b).astype(BF)
        self_off = jnp.stack([zero, jnp.int32(HALF), odd * HALF])
        self_live = jnp.stack([len_full, len_full, len_half])
        attended, stat_self = attn_fwd(
            query, pair, self_off, self_live,
            causal=True, bq=HALF, nq=3, q0=0, item_of=lambda j: j // 2, S=LEN, hb=3,
        )
        after_self = rows_in + mm(attended, output_w, NN) + output_bias.astype(F32)

        normal_cross, scaled_cross = norm_parts(after_self)
        second = norm_apply(normal_cross, cross_gain, cross_shift)
        lookup = (mm(second, lookup_t, NT) + lookup_b).astype(BF)
        heard_half = (mm(shared, source_w, NT) + source_bb).astype(BF)
        heard_full = (mm(full, source_w, NT) + source_bb).astype(BF)
        none = jnp.zeros((1,), jnp.int32)
        one_item = dict(causal=False, nq=1, item_of=lambda j: 0, S=frames)
        recalled_half, stat_half = attn_fwd(
            lookup, heard_half, none, live_half.reshape(1), bq=HALF, q0=2, hb=2, **one_item
        )
        recalled_full, stat_full = attn_fwd(
            lookup, heard_full, none, live_full.reshape(1), bq=LEN, q0=0, hb=3, **one_item
        )
        recalled = jnp.concatenate([recalled_full, recalled_half])
        after_cross = after_self + mm(recalled, merged_w, NN) + merged_bias.astype(F32)

        normal_dense, scaled_dense = norm_parts(after_cross)
        third = norm_apply(normal_dense, dense_gain, dense_shift)
        widened = mm(third, expand_t, NT) + expand_b
        below = 0.5 * (1.0 + lax.erf(widened * math.sqrt(0.5)))
        activated = (widened * below).astype(BF)
        slope = (
            below + widened * (jnp.exp(-0.5 * widened * widened) * (1.0 / math.sqrt(2.0 * math.pi)))
        ).astype(BF)
        result = (
            after_cross + mm(activated, reduce_w, NN) + reduce_bias.astype(F32)
        ).astype(BF)
        spread_dense = arrange(cotangent)
        grad_out = spread_dense.astype(F32)
        grad_reduce_bias = jnp.sum(grad_out, axis=0)
        grad_widened = (mm(spread_dense, reduce_w, NT) * slope.astype(F32)).astype(BF)
        grad_reduce = mm(activated, spread_dense, TN)
        grad_expand = mm(grad_widened, third, TN)
        grad_expand_bias = jnp.sum(grad_widened.astype(F32), axis=0)
        back_dense = mm(grad_widened, expand_t, NN)
        grad_dense_gain = jnp.sum(back_dense * normal_dense, axis=0)
        grad_dense_shift = jnp.sum(back_dense, axis=0)
        grad_after_cross = grad_out + norm_backward(
            back_dense, normal_dense, scaled_dense, dense_gain
        )

        def over_wide(values):
            share = values.shape[0] // wide
            pieces = lax.all_to_all(values, "wide", split_axis=0, concat_axis=0, tiled=True)
            total = jnp.sum(pieces.reshape(wide, share, width).astype(F32), axis=0)
            return lax.all_gather(total.astype(BF), "wide", axis=0, tiled=True).astype(F32)

        def over_all(values):
            return over_wide(
                lax.psum_scatter(values.astype(BF), "narrow", scatter_dimension=0, tiled=True)
            )

        def over_all_group(parts):
            count = len(parts)
            lined = jnp.stack([p.astype(BF).reshape(narrow, part, width) for p in parts], axis=1)
            summed = over_all(lined.reshape(narrow * count * part, width))
            return [summed[i * part : (i + 1) * part] for i in range(count)]

        sum_reduce = over_all(grad_reduce)
        sum_expand = over_all(grad_expand).T

        grad_merged_bias = jnp.sum(grad_after_cross, axis=0)
        spread_cross = grad_after_cross.astype(BF)
        grad_merged = mm(recalled, spread_cross, TN)
        grad_recalled = mm(spread_cross, merged_w, NT).astype(BF)
        back = dict(causal=False, nq=1, item_of=lambda j: 0, items=1, first=(0,), last=(0,), S=frames, s0=0)
        d_lookup_half, d_heard_half = attn_bwd(
            lookup, heard_half, grad_recalled, recalled, stat_half, none, live_half.reshape(1),
            bq=HALF, q0=2, do0=2, **back,
        )
        d_lookup_full, d_heard_full = attn_bwd(
            lookup, heard_full, grad_recalled, recalled, stat_full, none, live_full.reshape(1),
            bq=LEN, q0=0, do0=0, **back,
        )

        def leave(values):
            moved = spread(values.reshape(wide, own_frames, 2 * part))
            return moved[..., :part], pack(moved[..., part:])

        back_half = mm(d_heard_half, source_w, NN).astype(BF)
        shared_sum = (
            back_half[:, : 2 * part].astype(F32) + swap(back_half[:, 2 * part :]).astype(F32)
        ).astype(BF)
        shared_out = leave(shared_sum)
        back_full = mm(d_heard_full, source_w, NN).astype(BF)
        full_own = back_full[:, : 2 * part]
        full_got = swap(back_full[:, 2 * part :])
        first_out = leave(jnp.where(is_odd, full_got, full_own))
        last_out = leave(jnp.where(is_odd, full_own, full_got))
        outs = [first_out, shared_out, last_out]
        here = jnp.stack([o[0] for o in outs], axis=1)
        there = jnp.stack(
            [unpack(lax.ppermute(o[1], "narrow", across)) for o in outs], axis=1
        )
        low_chip = chip == 0
        encoded_grad = jnp.stack(
            [jnp.where(low_chip, here, there), jnp.where(low_chip, there, here)], axis=1
        ).reshape(encoded.shape)

        d_lookup = jnp.concatenate([d_lookup_full, d_lookup_half])
        grad_lookup_bias = jnp.sum(d_lookup.astype(F32), axis=0)
        grad_lookup = mm(d_lookup, second, TN)
        grad_source = mm(d_heard_full, full, TN) + mm(d_heard_half, shared, TN)
        grad_source = grad_source.astype(BF).reshape(2 * width, narrow, part)
        places = [n, n ^ 1, n ^ 2, n ^ 3]
        table = jnp.array([0, 2, 1, 3], jnp.int32)
        grad_source = jnp.concatenate(
            [
                lax.dynamic_index_in_dim(grad_source, table[n ^ i], 1, keepdims=False)
                for i in range(narrow)
            ],
            -1,
        )
        grad_keys, grad_values = separate(grad_source)
        sum_bias = jnp.sum(d_heard_full.astype(F32), axis=0) + jnp.sum(
            d_heard_half.astype(F32), axis=0
        )
        unused, grad_source_bias = separate(sum_bias)
        back_cross = mm(d_lookup, lookup_t, NN)
        grad_cross_gain = jnp.sum(back_cross * normal_cross, axis=0)
        grad_cross_shift = jnp.sum(back_cross, axis=0)
        grad_after_self = grad_after_cross + norm_backward(
            back_cross, normal_cross, scaled_cross, cross_gain
        )
        sum_lookup, sum_keys, sum_values, sum_merged = over_all_group(
            [grad_lookup, grad_keys, grad_values, grad_merged]
        )

        grad_output_bias = jnp.sum(grad_after_self, axis=0)
        spread_self = grad_after_self.astype(BF)
        grad_output = mm(attended, spread_self, TN)
        grad_attended = mm(spread_self, output_w, NT).astype(BF)
        d_query, d_pair = attn_bwd(
            query, pair, grad_attended, attended, stat_self, self_off, self_live,
            causal=True, bq=HALF, nq=3, q0=0, do0=0, s0=0, item_of=lambda j: j // 2,
            items=2, first=(0, 2), last=(1, 2), S=LEN, hb=3,
        )
        back_ext = mm(d_pair, pair_t, NN)
        near, far = back_ext[LEN : LEN + HALF], back_ext[LEN + HALF :]
        half_back = jnp.where(is_odd, far, near) + swap(jnp.where(is_odd, near, far))
        back_self = jnp.concatenate([back_ext[:LEN], half_back]) + mm(d_query, query_t, NN)
        grad_query_bias = jnp.sum(d_query.astype(F32), axis=0)
        unused, grad_value_bias = separate(jnp.sum(d_pair.astype(F32), axis=0))
        grad_query = mm(d_query, first, TN)
        grad_key, grad_value = separate(mm(d_pair, first_ext, TN))
        sum_query, sum_key, sum_value, sum_output = over_all_group(
            [grad_query, grad_key, grad_value, grad_output]
        )
        grad_attn_gain = jnp.sum(back_self * normal_self, axis=0)
        grad_attn_shift = jnp.sum(back_self, axis=0)
        tokens_grad = (
            grad_after_self + norm_backward(back_self, normal_self, scaled_self, attn_gain)
        ).astype(BF)

        small = lax.psum(
            jnp.concatenate(
                [
                    jnp.stack(
                        [
                            grad_attn_gain,
                            grad_attn_shift,
                            grad_output_bias,
                            grad_cross_gain,
                            grad_cross_shift,
                            grad_merged_bias,
                            grad_dense_gain,
                            grad_dense_shift,
                            grad_reduce_bias,
                            grad_query_bias,
                            grad_value_bias,
                            grad_lookup_bias,
                            grad_source_bias,
                        ]
                    ),
                    grad_expand_bias.reshape(-1, width),
                ]
            ),
            ("wide", "narrow"),
        )

        def own(vector):
            share = vector.shape[0] // narrow
            return lax.dynamic_slice_in_dim(vector, n * share, share)

        return (
            restore(result),
            restore(tokens_grad),
            encoded_grad,
            small[0],
            small[1],
            sum_query.T,
            own(small[9]),
            sum_key.T,
            sum_value.T,
            own(small[10]),
            sum_output,
            small[2],
            small[3],
            small[4],
            sum_lookup.T,
            own(small[11]),
            sum_keys.T,
            sum_values.T,
            own(small[12]),
            sum_merged,
            small[5],
            small[6],
            small[7],
            sum_expand,
            own(small[13:].reshape(-1)),
            sum_reduce,
            small[8],
        )

    return on_device


def solution(mesh):
    placed = (
        P(("wide", "narrow"), None),
        P(None, "wide", "narrow"),
        P("wide"),
        P("wide"),
        P(("wide", "narrow"), None),
        P(),
        P(),
        P(None, "narrow"),
        P("narrow"),
        P(None, "narrow"),
        P(None, "narrow"),
        P("narrow"),
        P("narrow", None),
        P(),
        P(),
        P(),
        P(None, "narrow"),
        P("narrow"),
        P(None, "narrow"),
        P(None, "narrow"),
        P("narrow"),
        P("narrow", None),
        P(),
        P(),
        P(),
        P(None, "narrow"),
        P("narrow"),
        P("narrow", None),
        P(),
    )
    return jax.shard_map(
        make_body(mesh.shape["wide"], mesh.shape["narrow"]),
        mesh=mesh,
        in_specs=placed,
        out_specs=(
            P(("wide", "narrow"), None),
            P(("wide", "narrow"), None),
            P(None, "wide", "narrow"),
            P(),
            P(),
            P(None, "narrow"),
            P("narrow"),
            P(None, "narrow"),
            P(None, "narrow"),
            P("narrow"),
            P("narrow", None),
            P(),
            P(),
            P(),
            P(None, "narrow"),
            P("narrow"),
            P(None, "narrow"),
            P(None, "narrow"),
            P("narrow"),
            P("narrow", None),
            P(),
            P(),
            P(),
            P(None, "narrow"),
            P("narrow"),
            P("narrow", None),
            P(),
        ),
        check_vma=False,
    )
```
